32 devices in a mesh: probe: 8 (over y, x, core), tile: 4 (over z).
Axes of the slice: x: 2, y: 2, z: 4, core: 2. Of those that a mesh axis runs over, the one named last changes fastest.
Arguments:
- transmission: bfloat16 [2, 2, 2048, 1024], P(None, None, 'tile', 'probe'), may hold values from -4.1875 to 4.1875
- illumination: bfloat16 [2, 512, 512], replicated, may hold values from -3 to 3
- intensities: float32 [16, 512, 512], P('probe'), may hold values from 0 to 1
- scan_positions: int32 [16, 2], P('probe'), may hold values from 0 to 512, as said below
- tile_owner: int32 [16], P('probe'), may hold values from 0 to 3, as said below
Outputs:
- gradient: float32 [2, 2, 2048, 1024], P(None, None, 'tile', 'probe')
- probe_losses: float32 [16], P('probe')
The draws below stay inside these ranges and needn't reach their ends.
Inputs may be any that keep to these rules, and one draw needn't show every extreme that they name: `tile_owner`: of the 2 scan positions held by one device along probe, no two have the same owner. scan_positions[k, 0] counts rows from row tile_owner[k] * 512 - 128 of the object and scan_positions[k, 1] columns from its first column; the 512 x 512 window of every probe lies inside the object and inside its owner's rows widened by 128 on each side.
All inputs are finite; a program needn't handle non-finite values.
Results may differ from the reference program's by a relative error of at most 0.012.
Values may be sent and summed in bfloat16 or wider, within the bound.
A program may use at most 128 MiB of HBM per device.

```python
import math
import jax
import jax.numpy as jnp
from jax import lax

SLICES = 2
FRAME = 512
BORDER = 128
TILE_ROWS = 512
OBJ_COLS = 1024
PR_DEV = 2
CAP = 1
PROBES = 16
OBJ_ROWS = 2048
N_TILE = 4


def owners_and_places(key):
    base_key = jax.random.fold_in(key, 11)
    subkeys = jax.random.split(base_key, 5)
    shards = PROBES // PR_DEV
    leading = jax.random.randint(subkeys[0], (shards, 1), 0, N_TILE)
    others = (leading + 1 + jax.random.randint(subkeys[1], (shards, PR_DEV - CAP), 0, N_TILE - 1)) % N_TILE
    owners = jnp.concatenate([jnp.broadcast_to(leading, (shards, CAP)), others], axis=1)
    scores = jax.random.randint(subkeys[2], (shards, PR_DEV), 0, 1 << 20) * PR_DEV + jnp.arange(PR_DEV)
    ranking = jnp.argsort(scores, axis=1)
    owners = jnp.take_along_axis(owners, ranking, axis=1).reshape(PROBES)
    local_rows = jax.random.randint(subkeys[3], (PROBES,), 0, TILE_ROWS + 2 * BORDER - FRAME + 1)
    global_rows = jnp.clip(owners * TILE_ROWS - BORDER + local_rows, 0, OBJ_ROWS - FRAME)
    local_rows = global_rows - owners * TILE_ROWS + BORDER
    columns = jax.random.randint(subkeys[4], (PROBES,), 0, OBJ_COLS - FRAME + 1)
    places = jnp.stack([local_rows, columns], axis=1)
    return (owners.astype(jnp.int32), places.astype(jnp.int32))


def draw_tile_owner(key, part):
    return owners_and_places(key)[0]


def draw_scan_positions(key, part):
    return owners_and_places(key)[1]


def block_scale(own_key, dims, cuts, least, largest):
    def one(dim, blocks):
        heights = jax.random.uniform(jax.random.fold_in(jax.random.fold_in(own_key, 6), dim), (blocks,), jnp.float32, least / len(cuts), largest / len(cuts))
        return jnp.repeat(jnp.exp(heights), dims[dim] // blocks).reshape((-1,) + (1,) * (len(dims) - dim - 1))

    factor_of = one(*cuts[0])
    for cut in cuts[1:]:
        factor_of = factor_of * one(*cut)
    return factor_of


def gaussian(own_key, dims, deviation, limit, pieces=(), kind=jnp.bfloat16):
    factor_of = block_scale(own_key, dims, pieces, -0.22, 0.18) if pieces else 1.0
    drawn = jax.random.normal(own_key, dims, jnp.float32) * deviation * factor_of
    return jnp.minimum(jnp.maximum(drawn, -limit), limit).astype(kind)


def setup_inputs(seed: int = 0) -> dict:
    arg_keys = jax.random.split(jax.random.key(seed), 6)
    transmission = gaussian(arg_keys[0], (SLICES, 2, OBJ_ROWS, OBJ_COLS), 0.7, 4.1875, ((2, 4), (3, 8)))
    illumination = gaussian(arg_keys[1], (2, FRAME, FRAME), 0.5, 3.0)
    intensities = jnp.clip(1.0 * jax.random.uniform(arg_keys[2], (PROBES, FRAME, FRAME), jnp.float32) ** block_scale(arg_keys[2], (PROBES, FRAME, FRAME), ((0, 8),), -0.2, 0.2), 0.0, 1.0)
    scan_positions = draw_scan_positions(jax.random.fold_in(arg_keys[5], 71), 0)
    tile_owner = draw_tile_owner(jax.random.fold_in(arg_keys[5], 71), 0)
    return {"transmission": transmission, "illumination": illumination, "intensities": intensities, "scan_positions": scan_positions, "tile_owner": tile_owner}


fresnel = 0.25

def build_tables(frame_size):
    indices = jnp.arange(frame_size, dtype=jnp.int32)
    product = indices[:, None] * indices[None, :] % frame_size
    angle = -2.0 * math.pi * product.astype(jnp.float32) / frame_size
    norming = 1.0 / math.sqrt(frame_size)
    dft_re = jnp.cos(angle) * norming
    dft_im = jnp.sin(angle) * norming
    freq = jnp.where(indices < frame_size // 2, indices, indices - frame_size).astype(jnp.float32)
    phase = -math.pi * fresnel * freq * freq / frame_size
    kernel_re = jnp.cos(phase)[:, None]
    kernel_im = jnp.sin(phase)[:, None]
    scaled_re = kernel_re * dft_re - kernel_im * dft_im
    scaled_im = kernel_re * dft_im + kernel_im * dft_re
    high = lax.Precision.HIGHEST
    prop_re = jnp.dot(dft_re, scaled_re, precision=high) + jnp.dot(dft_im, scaled_im, precision=high)
    prop_im = jnp.dot(dft_re, scaled_im, precision=high) - jnp.dot(dft_im, scaled_re, precision=high)
    wave_re = dft_re.astype(jnp.bfloat16)
    wave_im = dft_im.astype(jnp.bfloat16)
    qmat_re = prop_re.astype(jnp.bfloat16)
    qmat_im = prop_im.astype(jnp.bfloat16)
    prop_tables = (qmat_re, qmat_im, qmat_re.T, qmat_im.T)
    prop_adjoint = (qmat_re.T, -qmat_im.T, qmat_re, -qmat_im)
    far_tables = (wave_re, wave_im, wave_re, wave_im)
    far_adjoint = (wave_re, -wave_im, wave_re, -wave_im)
    return (prop_tables, prop_adjoint, far_tables, far_adjoint)

def complex_dot(left_re, left_im, right_re, right_im):
    real_part = jnp.dot(left_re, right_re, preferred_element_type=jnp.float32) - jnp.dot(left_im, right_im, preferred_element_type=jnp.float32)
    imag_part = jnp.dot(left_re, right_im, preferred_element_type=jnp.float32) + jnp.dot(left_im, right_re, preferred_element_type=jnp.float32)
    return (real_part, imag_part)

def transform(field_re, field_im, table):
    left_re, left_im, right_re, right_im = table
    inner_re, inner_im = complex_dot(field_re.astype(jnp.bfloat16), field_im.astype(jnp.bfloat16), right_re, right_im)
    return complex_dot(left_re, left_im, inner_re.astype(jnp.bfloat16), inner_im.astype(jnp.bfloat16))

def probe_pass(patch, measured, illumination, tables):
    prop_tables, prop_adjoint, far_tables, far_adjoint = tables
    slice_count = patch.shape[0]
    wave_re = illumination[0].astype(jnp.float32)
    wave_im = illumination[1].astype(jnp.float32)
    inputs = []
    for slice_index in range(slice_count):
        inputs.append((wave_re, wave_im))
        layer_re = patch[slice_index, 0].astype(jnp.float32)
        layer_im = patch[slice_index, 1].astype(jnp.float32)
        exit_re = wave_re * layer_re - wave_im * layer_im
        exit_im = wave_re * layer_im + wave_im * layer_re
        if slice_index < slice_count - 1:
            wave_re, wave_im = transform(exit_re, exit_im, prop_tables)
        else:
            far_re, far_im = transform(exit_re, exit_im, far_tables)
    misfit = far_re * far_re + far_im * far_im - measured
    loss_value = jnp.mean(misfit * misfit)
    back_re, back_im = transform(misfit * far_re, misfit * far_im, far_adjoint)
    grad_list = [None] * slice_count
    for slice_index in range(slice_count - 1, -1, -1):
        wave_re, wave_im = inputs[slice_index]
        grad_re = wave_re * back_re + wave_im * back_im
        grad_im = wave_re * back_im - wave_im * back_re
        grad_list[slice_index] = jnp.stack([grad_re, grad_im])
        if slice_index > 0:
            layer_re = patch[slice_index, 0].astype(jnp.float32)
            layer_im = patch[slice_index, 1].astype(jnp.float32)
            carry_re = layer_re * back_re + layer_im * back_im
            carry_im = layer_re * back_im - layer_im * back_re
            back_re, back_im = transform(carry_re, carry_im, prop_adjoint)
    return (jnp.stack(grad_list), loss_value)

def reference(transmission, illumination, intensities, scan_positions, tile_owner):
    tables = build_tables(FRAME)
    zero_index = jnp.zeros((), jnp.int32)
    initial = jnp.zeros((SLICES, 2, OBJ_ROWS, OBJ_COLS), jnp.float32)

    def visit(summed, item):
        measured, position, owner = item
        row_start = (owner * TILE_ROWS - BORDER + position[0]).astype(jnp.int32)
        col_start = position[1].astype(jnp.int32)
        starts = (zero_index, zero_index, row_start, col_start)
        patch = lax.dynamic_slice(transmission, starts, (SLICES, 2, FRAME, FRAME))
        patch_grad, loss_value = probe_pass(patch, measured, illumination, tables)
        current = lax.dynamic_slice(summed, starts, (SLICES, 2, FRAME, FRAME))
        summed = lax.dynamic_update_slice(summed, current + patch_grad, starts)
        return (summed, loss_value)
    gradient, probe_losses = lax.scan(visit, initial, (intensities, scan_positions, tile_owner))
    return (gradient, probe_losses)
```

```python
import functools
import math

import jax
import jax.numpy as jnp
import numpy as np
from jax import lax
from jax.experimental import pallas as pl
from jax.experimental.pallas import tpu as pltpu
from jax.sharding import PartitionSpec as P

BORDER = 128
FRESNEL = 0.25
F32 = jnp.float32
BF16 = jnp.bfloat16


def tables_of(n):
    k = np.arange(n)
    angle = -2.0 * np.pi * ((k[:, None] * k[None, :]) % n) / n
    wave = np.exp(1j * angle) / math.sqrt(n)
    freq = np.where(k < n // 2, k, k - n).astype(np.float64)
    h = np.exp(-1j * np.pi * FRESNEL * freq * freq / n)
    q = np.fft.ifft(h)
    prop = q[(k[:, None] - k[None, :]) % n]
    return [jnp.asarray(np.asarray(t, np.float32).astype(jnp.bfloat16))
            for t in (wave.real, wave.imag, prop.real, prop.imag)]


def compute_kernel(pos, band, illum, meas, wr, wi, qr, qi, out, loss,
                   wide, x0, x1, obj, er, ei, ir, ii, msc, msem):
    n = illum.shape[-1]
    slices = band.shape[0]
    assert slices == 2
    step = n // 2
    row0, col0, usable, chosen = pos[0], pos[1], pos[2], pos[3]
    extra = band.shape[2] - n

    @pl.when(usable == 0)
    def _():
        loss[...] = jnp.zeros_like(loss)
        for s in range(slices):
            for c in range(2):
                out[s, c] = jnp.zeros(out.shape[2:], out.dtype)

    def chunks(fn):
        def body(i, carry):
            fn(pl.multiple_of(i * step, step))
            return carry
        lax.fori_loop(0, n // step, body, 0)

    def transform(tr, ti, sign, emit):
        def right(r):
            a, b = er[pl.ds(r, step), :], ei[pl.ds(r, step), :]
            dot = functools.partial(jnp.dot, preferred_element_type=F32)
            rr, mm = dot(a, tr[...]), dot(b, ti[...])
            ir[pl.ds(r, step), :] = (rr - mm if sign > 0 else rr + mm).astype(BF16)
            rm, mr = dot(a, ti[...]), dot(b, tr[...])
            ii[pl.ds(r, step), :] = (mr + rm if sign > 0 else mr - rm).astype(BF16)

        chunks(right)

        def left(r):
            a, b = tr[pl.ds(r, step), :], ti[pl.ds(r, step), :]
            dot = functools.partial(jnp.dot, preferred_element_type=F32)
            rr, mm = dot(a, ir[...]), dot(b, ii[...])
            rm, mr = dot(a, ii[...]), dot(b, ir[...])
            emit(r, rr - mm if sign > 0 else rr + mm, rm + mr if sign > 0 else rm - mr)

        chunks(left)

    @pl.when(usable != 0)
    def _():
        fetch = pltpu.make_async_copy(meas.at[chosen], msc, msem)
        fetch.start()
        for c in range(2):
            for r in range(0, n, 64):
                turned = pltpu.roll(illum[c, r:r + 64, :].astype(F32), col0 & (n - 1), 1)
                wide[r:r + 64, :] = turned
                wide[n + r:n + r + 64, :] = turned
            base = (n - row0) // 8 * 8
            turn = (72 - (n - row0 - base)) % 72
            for r in range(0, n, 64):
                lines = wide[pl.ds(pl.multiple_of(base + r, 8), 72), :]
                x0[c, r:r + 64, :] = pltpu.roll(lines, turn, 0)[:64]

        col = lax.broadcasted_iota(jnp.int32, (64, n), 1)
        line = lax.broadcasted_iota(jnp.int32, (64, n), 0)
        for s in range(slices):
            for r in range(0, n, 64):
                part = []
                for c in range(2):
                    low = jnp.where(col < col0, band[s, c, r:r + 64, n:].astype(F32),
                                    band[s, c, r:r + 64, :n].astype(F32))
                    if r < extra:
                        high = jnp.where(col < col0, band[s, c, n + r:n + r + 64, n:].astype(F32),
                                         band[s, c, n + r:n + r + 64, :n].astype(F32))
                        low = jnp.where(line + r < row0, high, low)
                    part.append(low)
                a, b = part
                if s == 0:
                    u, v = x0[0, r:r + 64, :], x0[1, r:r + 64, :]
                    er[r:r + 64, :] = (u * a - v * b).astype(BF16)
                    ei[r:r + 64, :] = (u * b + v * a).astype(BF16)
                else:
                    obj[0, r:r + 64, :] = a.astype(BF16)
                    obj[1, r:r + 64, :] = b.astype(BF16)

        def emit_first(r, re, im):
            rows = pl.ds(r, step)
            x1[0, rows, :] = re
            x1[1, rows, :] = im
            a, b = obj[0, rows, :].astype(F32), obj[1, rows, :].astype(F32)
            er[rows, :] = (re * a - im * b).astype(BF16)
            ei[rows, :] = (re * b + im * a).astype(BF16)

        transform(qr, qi, 1, emit_first)
        fetch.wait()
        loss[...] = jnp.zeros_like(loss)

        def emit_far(r, re, im):
            rows = pl.ds(r, step)
            misfit = re * re + im * im - msc[rows, :]
            sq = jnp.sum((misfit * misfit).reshape(step // 8, 8, n), axis=0)
            loss[...] += functools.reduce(jnp.add, [sq[:, j:j + 128] for j in range(0, n, 128)])
            er[rows, :] = (misfit * re).astype(BF16)
            ei[rows, :] = (misfit * im).astype(BF16)

        transform(wr, wi, 1, emit_far)

        def place(s, r, parts):
            col = lax.broadcasted_iota(jnp.int32, (step, n), 1)
            line = lax.broadcasted_iota(jnp.int32, (step, n), 0) + r
            for c, g in enumerate(parts):
                keep = jnp.where(line >= row0, g, 0.0)
                out[s, c, pl.ds(r, step), :n] = jnp.where(col >= col0, keep, 0.0).astype(BF16)
                out[s, c, pl.ds(r, step), n:] = jnp.where(col < col0, keep, 0.0).astype(BF16)

                @pl.when(r < extra)
                def _():
                    for j in range(0, extra, step):
                        over = jnp.where(line < row0, g, 0.0)
                        out[s, c, n + j:n + j + step, :n] = jnp.where(col >= col0, over, 0.0).astype(BF16)
                        out[s, c, n + j:n + j + step, n:] = jnp.where(col < col0, over, 0.0).astype(BF16)

        def emit_back(r, re, im):
            rows = pl.ds(r, step)
            u, v = x1[0, rows, :], x1[1, rows, :]
            place(1, r, (u * re + v * im, u * im - v * re))
            a, b = obj[0, rows, :].astype(F32), obj[1, rows, :].astype(F32)
            er[rows, :] = (a * re + b * im).astype(BF16)
            ei[rows, :] = (a * im - b * re).astype(BF16)

        transform(wr, wi, -1, emit_back)

        def emit_last(r, re, im):
            rows = pl.ds(r, step)
            u, v = x0[0, rows, :], x0[1, rows, :]
            place(0, r, (u * re + v * im, u * im - v * re))

        transform(qr, qi, -1, emit_last)


def compute(pos, band, illumination, intensities):
    n = illumination.shape[-1]
    vmem = pl.BlockSpec(memory_space=pltpu.VMEM)
    return pl.pallas_call(
        compute_kernel,
        out_shape=(jax.ShapeDtypeStruct(band.shape, BF16), jax.ShapeDtypeStruct((8, 128), F32)),
        in_specs=[pl.BlockSpec(memory_space=pltpu.SMEM), vmem, vmem,
                  pl.BlockSpec(memory_space=pl.ANY)] + [vmem] * 4,
        out_specs=(vmem, vmem),
        scratch_shapes=[
            pltpu.VMEM((2 * n + 8, n), F32), pltpu.VMEM((2, n, n), F32), pltpu.VMEM((2, n, n), F32),
            pltpu.VMEM((2, n, n), BF16)] + [pltpu.VMEM((n, n), BF16)] * 4 + [
            pltpu.VMEM((n, n), F32), pltpu.SemaphoreType.DMA],
        compiler_params=pltpu.CompilerParams(vmem_limit_bytes=56 << 20),
        name="probe_pass",
    )(pos, band, illumination, intensities, *tables_of(n))


def extended(value, axis, dim, width):
    size, length = lax.axis_size(axis), value.shape[dim]
    up = [(i, i + 1) for i in range(size - 1)]
    down = [(j, i) for i, j in up]
    before = lax.ppermute(lax.slice_in_dim(value, length - width, length, axis=dim), axis, up)
    after = lax.ppermute(lax.slice_in_dim(value, 0, width, axis=dim), axis, down)
    return jnp.concatenate([before, value, after], axis=dim)


def body(transmission, illumination, intensities, scan_positions, tile_owner):
    tile_index = lax.axis_index("tile")
    tile_rows = transmission.shape[2]
    n = illumination.shape[-1]
    owned = tile_owner == tile_index
    chosen = jnp.argmax(owned).astype(jnp.int32)
    usable = jnp.any(owned)
    place = jnp.sum(jnp.where(owned[:, None], scan_positions, 0), axis=0)
    pos = jnp.stack([place[0], place[1], usable.astype(jnp.int32), chosen])
    band = lax.all_gather(extended(transmission, "tile", 2, BORDER), "probe", axis=3, tiled=True)
    summed, loss = compute(pos, band, illumination, intensities)
    wide = lax.psum_scatter(summed, "probe", scatter_dimension=3, tiled=True).astype(F32)
    size = lax.axis_size("tile")
    up = [(i, i + 1) for i in range(size - 1)]
    down = [(j, i) for i, j in up]
    from_above = lax.ppermute(wide[:, :, :BORDER].astype(BF16), "tile", down).astype(F32)
    from_below = lax.ppermute(wide[:, :, tile_rows + BORDER:].astype(BF16), "tile", up).astype(F32)
    interior = wide[:, :, BORDER:BORDER + tile_rows]
    interior = interior.at[:, :, tile_rows - BORDER:].add(from_above)
    interior = interior.at[:, :, :BORDER].add(from_below)
    local = jnp.where(owned, jnp.sum(loss) / (n * n), 0.0)
    return interior, lax.psum(local, "tile")


def solution(mesh):
    in_specs = (P(None, None, "tile", "probe"), P(), P("probe", None, None), P("probe", None), P("probe"))
    out_specs = (P(None, None, "tile", "probe"), P("probe"))
    return jax.shard_map(body, mesh=mesh, in_specs=in_specs, out_specs=out_specs, check_vma=False)
```

```python
import functools
import math

import jax
import jax.numpy as jnp
import numpy as np
from jax import lax
from jax.experimental import pallas as pl
from jax.experimental.pallas import tpu as pltpu
from jax.sharding import PartitionSpec as P

BORDER = 128
FRESNEL = 0.25
F32 = jnp.float32
BF16 = jnp.bfloat16


def tables_of(n):
    k = np.arange(n)
    angle = -2.0 * np.pi * ((k[:, None] * k[None, :]) % n) / n
    wave = np.exp(1j * angle) / math.sqrt(n)
    freq = np.where(k < n // 2, k, k - n).astype(np.float64)
    h = np.exp(-1j * np.pi * FRESNEL * freq * freq / n)
    q = np.fft.ifft(h)
    prop = q[(k[:, None] - k[None, :]) % n]
    return [jnp.asarray(np.asarray(t, np.float32).astype(jnp.bfloat16))
            for t in (wave.real, wave.imag, prop.real, prop.imag)]


def compute_kernel(pos, fold, illum, meas, wr, wi, qr, qi, out, loss,
                   wide, x0, x1, obj, er, ei, ir, ii, msc, msem):
    n = illum.shape[-1]
    blocks, slices, width = fold.shape[0], fold.shape[1], fold.shape[-1]
    assert slices == 2
    step = n // 2
    row0, col0, usable, chosen = pos[0], pos[1], pos[2], pos[3]

    @pl.when(usable == 0)
    def _():
        loss[...] = jnp.zeros_like(loss)
        out[...] = jnp.zeros_like(out)

    def chunks(fn):
        def body(i, carry):
            fn(pl.multiple_of(i * step, step))
            return carry
        lax.fori_loop(0, n // step, body, 0)

    def transform(tr, ti, sign, emit):
        dot = functools.partial(jnp.dot, preferred_element_type=F32)

        def right(r):
            a, b = er[pl.ds(r, step), :], ei[pl.ds(r, step), :]
            rr, mm = dot(a, tr[...]), dot(b, ti[...])
            ir[pl.ds(r, step), :] = (rr - mm if sign > 0 else rr + mm).astype(BF16)
            rm, mr = dot(a, ti[...]), dot(b, tr[...])
            ii[pl.ds(r, step), :] = (mr + rm if sign > 0 else mr - rm).astype(BF16)

        chunks(right)

        def left(r):
            a, b = tr[pl.ds(r, step), :], ti[pl.ds(r, step), :]
            rr, mm = dot(a, ir[...]), dot(b, ii[...])
            rm, mr = dot(a, ii[...]), dot(b, ir[...])
            emit(r, rr - mm if sign > 0 else rr + mm, rm + mr if sign > 0 else rm - mr)

        chunks(left)

    @pl.when(usable != 0)
    def _():
        fetch = pltpu.make_async_copy(meas.at[chosen], msc, msem)
        fetch.start()
        wide[2 * n:, :] = jnp.zeros((8, n), F32)
        base = (n - row0) // 8 * 8
        turn = (72 - (n - row0 - base)) % 72
        for c in range(2):
            for r in range(0, n, 64):
                turned = pltpu.roll(illum[c, r:r + 64, :].astype(F32), col0 & (n - 1), 1)
                wide[r:r + 64, :] = turned
                wide[n + r:n + r + 64, :] = turned
            for r in range(0, n, 64):
                lines = wide[pl.ds(pl.multiple_of(base + r, 8), 72), :]
                x0[c, r:r + 64, :] = pltpu.roll(lines, turn, 0)[:64]

        for j in range(blocks):
            cols = slice(j * width, (j + 1) * width)
            for r in range(0, n, 128):
                rows = slice(r, r + 128)
                a, b = fold[j, 0, 0, rows].astype(F32), fold[j, 0, 1, rows].astype(F32)
                u, v = x0[0, rows, cols], x0[1, rows, cols]
                er[rows, cols] = (u * a - v * b).astype(BF16)
                ei[rows, cols] = (u * b + v * a).astype(BF16)
            obj[:, :, cols] = fold[j, 1]

        def emit_first(r, re, im):
            rows = pl.ds(r, step)
            x1[0, rows, :] = re
            x1[1, rows, :] = im
            a, b = obj[0, rows, :].astype(F32), obj[1, rows, :].astype(F32)
            er[rows, :] = (re * a - im * b).astype(BF16)
            ei[rows, :] = (re * b + im * a).astype(BF16)

        transform(qr, qi, 1, emit_first)
        fetch.wait()
        loss[...] = jnp.zeros_like(loss)

        def emit_far(r, re, im):
            rows = pl.ds(r, step)
            misfit = re * re + im * im - msc[rows, :]
            sq = jnp.sum((misfit * misfit).reshape(step // 8, 8, n), axis=0)
            loss[...] += functools.reduce(jnp.add, [sq[:, j:j + 128] for j in range(0, n, 128)])
            er[rows, :] = (misfit * re).astype(BF16)
            ei[rows, :] = (misfit * im).astype(BF16)

        transform(wr, wi, 1, emit_far)
        slot = lax.broadcasted_iota(jnp.int32, loss.shape, 0)
        loss[...] = jnp.where(slot == chosen, jnp.sum(loss[...]) / (n * n), 0.0)

        def place(s, r, parts):
            for c, g in enumerate(parts):
                for j in range(blocks):
                    out[j, s, c, pl.ds(r, step), :] = g[:, j * width:(j + 1) * width].astype(BF16)

        def emit_back(r, re, im):
            rows = pl.ds(r, step)
            u, v = x1[0, rows, :], x1[1, rows, :]
            place(1, r, (u * re + v * im, u * im - v * re))
            a, b = obj[0, rows, :].astype(F32), obj[1, rows, :].astype(F32)
            er[rows, :] = (a * re + b * im).astype(BF16)
            ei[rows, :] = (a * im - b * re).astype(BF16)

        transform(wr, wi, -1, emit_back)

        def emit_last(r, re, im):
            rows = pl.ds(r, step)
            u, v = x0[0, rows, :], x0[1, rows, :]
            place(0, r, (u * re + v * im, u * im - v * re))

        transform(qr, qi, -1, emit_last)


def compute(pos, fold, illumination, intensities):
    n = illumination.shape[-1]
    vmem = pl.BlockSpec(memory_space=pltpu.VMEM)
    return pl.pallas_call(
        compute_kernel,
        out_shape=(jax.ShapeDtypeStruct(fold.shape, BF16), jax.ShapeDtypeStruct((8, 128), F32)),
        in_specs=[pl.BlockSpec(memory_space=pltpu.SMEM), vmem, vmem,
                  pl.BlockSpec(memory_space=pl.ANY)] + [vmem] * 4,
        out_specs=(vmem, vmem),
        scratch_shapes=[
            pltpu.VMEM((2 * n + 8, n), F32), pltpu.VMEM((2, n, n), F32), pltpu.VMEM((2, n, n), F32),
            pltpu.VMEM((2, n, n), BF16)] + [pltpu.VMEM((n, n), BF16)] * 4 + [
            pltpu.VMEM((n, n), F32), pltpu.SemaphoreType.DMA],
        compiler_params=pltpu.CompilerParams(vmem_limit_bytes=40 << 20),
        name="probe_pass",
    )(pos, fold, illumination, intensities, *tables_of(n))


MESH = pl.DeviceIdType.MESH


class Places:
    def __init__(self, group):
        self.group, self.tiles = group, lax.axis_size("tile")
        self.me, self.tile = lax.axis_index("probe"), lax.axis_index("tile")
        self.half, self.block = self.me // group, lax.rem(self.me, group)
        self.partner = (lax.rem(self.me + group, 2 * group), self.tile)

    def peer(self, off):
        return (self.half * self.group + lax.rem(self.block + off, self.group), self.tile)

    def tile_peer(self, off):
        return (self.me, lax.rem(self.tile + off, self.tiles))

    def meet(self):
        barrier = pltpu.get_barrier_semaphore()
        others = ([self.partner] + [self.peer(o) for o in range(1, self.group)]
                  + [self.tile_peer(o) for o in range(1, self.tiles)])
        for other in others:
            pl.semaphore_signal(barrier, inc=1, device_id=other, device_id_type=MESH)
        pl.semaphore_wait(barrier, len(others))


def remote(src, dst, send, recv, device):
    return pltpu.make_async_remote_copy(src_ref=src, dst_ref=dst, send_sem=send, recv_sem=recv,
                                        device_id=device, device_id_type=MESH)


def collect_kernel(group, tr, pos, fold, posall, ext, sbuf, psend, precv, zsend, zrecv,
                   ysend, yrecv, xsend, xrecv):
    slices, _, rows, width = tr.shape
    n = fold.shape[-2]
    extra = 2 * BORDER
    at = Places(group)
    at.meet()
    pcopies = [remote(pos, posall.at[o], psend.at[o], precv.at[o], at.peer(o)) for o in range(1, group)]
    for copy in pcopies:
        copy.start()
    top, low = slice(0, BORDER), slice(BORDER + rows, BORDER + rows + BORDER)
    mid = slice(BORDER, BORDER + rows)
    down = remote(tr.at[:, :, rows - BORDER:], ext.at[:, 0, :, top], zsend.at[0], zrecv.at[0], at.tile_peer(1))
    up = remote(tr.at[:, :, :BORDER], ext.at[:, 0, :, low], zsend.at[1], zrecv.at[1], at.tile_peer(at.tiles - 1))
    first, last = at.tile == 0, at.tile == at.tiles - 1

    @pl.when(jnp.logical_not(last))
    def _():
        down.start()

    @pl.when(jnp.logical_not(first))
    def _():
        up.start()

    ymid = [remote(tr.at[s], ext.at[s, 1, :, mid], ysend.at[s, 0], yrecv.at[s, 0], at.partner)
            for s in range(slices)]
    ymid[0].start()
    posall[0] = pos[...]
    for s in range(slices):
        ext[s, 0, :, mid, :] = tr[s]

    @pl.when(first)
    def _():
        ext[:, 0, :, top, :] = jnp.zeros((slices, 2, BORDER, width), BF16)

    @pl.when(last)
    def _():
        ext[:, 0, :, low, :] = jnp.zeros((slices, 2, BORDER, width), BF16)

    @pl.when(jnp.logical_not(first))
    def _():
        down.wait_recv()

    @pl.when(jnp.logical_not(last))
    def _():
        up.wait_recv()

    yends = []
    for s in range(slices):
        if s:
            ymid[s].start()
        pair = [remote(ext.at[s, 0, :, part], ext.at[s, 1, :, part], ysend.at[s, 1 + i], yrecv.at[s, 1 + i], at.partner)
                for i, part in enumerate((top, low))]
        for copy in pair:
            copy.start()
        yends.append(pair)
    for copy in pcopies:
        copy.wait_recv()
    lane = lax.broadcasted_iota(jnp.int32, (extra, width), 1) + at.block * width
    line = lax.broadcasted_iota(jnp.int32, (extra, width), 0)
    xcopies = []
    for s in range(slices):
        for copy in (ymid[s], *yends[s]):
            copy.wait_recv()
        for o in list(range(1, group)) + [0]:
            who = posall[(group - o) % group]
            row0, col0 = who[0:1, :width], who[1:2, :width]
            mine = jnp.where(lane < col0, 1, 0) == at.half
            for c in range(2):
                for r in range(0, n, extra):
                    v = jnp.where(mine, ext[s, 0, c, r:r + extra].astype(F32), ext[s, 1, c, r:r + extra].astype(F32))
                    if r + n < rows + extra:
                        w = jnp.where(mine, ext[s, 0, c, n + r:n + r + extra].astype(F32),
                                      ext[s, 1, c, n + r:n + r + extra].astype(F32))
                        v = jnp.where(line + r < row0, w, v)
                    if o:
                        sbuf[s, o, c, r:r + extra, :] = v.astype(BF16)
                    else:
                        fold[at.block, s, c, r:r + extra, :] = v.astype(BF16)
            if o:
                copy = remote(sbuf.at[s, o], fold.at[at.block, s], xsend.at[s, o], xrecv.at[s, o], at.peer(o))
                copy.start()
                xcopies.append(copy)
    for copy in pcopies + xcopies:
        copy.wait_send()
    for copy in xcopies:
        copy.wait_recv()
    for s in range(slices):
        for copy in (ymid[s], *yends[s]):
            copy.wait_send()

    @pl.when(jnp.logical_not(last))
    def _():
        down.wait_send()

    @pl.when(jnp.logical_not(first))
    def _():
        up.wait_send()


def collect(transmission, postile, n):
    slices, _, rows, width = transmission.shape
    group = n // width
    vmem = pl.BlockSpec(memory_space=pltpu.VMEM)
    dma = pltpu.SemaphoreType.DMA
    return pl.pallas_call(
        functools.partial(collect_kernel, group),
        out_shape=(jax.ShapeDtypeStruct((group, slices, 2, n, width), BF16),
                   jax.ShapeDtypeStruct((group, 8, 128), jnp.int32)),
        in_specs=[vmem, vmem], out_specs=(vmem, vmem),
        scratch_shapes=[
            pltpu.VMEM((slices, 2, 2, rows + 2 * BORDER, width), BF16),
            pltpu.VMEM((slices, group, 2, n, width), BF16),
            dma((group,)), dma((group,)), dma((2,)), dma((2,)), dma((slices, 3)), dma((slices, 3)),
            dma((slices, group)), dma((slices, group))],
        compiler_params=pltpu.CompilerParams(collective_id=0, has_side_effects=True, vmem_limit_bytes=24 << 20),
        name="collect",
    )(transmission, postile)


def spread_kernel(group, grad, posall, loss, out, losses, rbuf, keep, sbuf, ybuf, zout, zin, lbuf,
                  lsend, lrecv, zsend, zrecv, ysend, yrecv, xsend, xrecv):
    slices, _, rows, width = out.shape
    n = grad.shape[-2]
    at = Places(group)
    at.meet()
    order = list(range(slices - 1, -1, -1))
    xcopies = {}
    for s in order:
        for o in range(1, group):
            peer = lax.rem(at.block + o, group)
            xcopies[s, o] = remote(grad.at[peer, s], rbuf.at[s, o], xsend.at[s, o], xrecv.at[s, o], at.peer(o))
            xcopies[s, o].start()
    lcopies = [remote(loss, lbuf.at[o], lsend.at[o], lrecv.at[o], at.tile_peer(o)) for o in range(1, at.tiles)]
    for copy in lcopies:
        copy.start()
    lane = lax.broadcasted_iota(jnp.int32, (BORDER, width), 1) + at.block * width
    line = lax.broadcasted_iota(jnp.int32, (BORDER, width), 0)
    ycopies = {}
    for s in order:
        for o in range(1, group):
            xcopies[s, o].wait_recv()
        for away in (True, False):
            cols = lane + (1 - at.half if away else at.half) * n
            for c in range(2):
                for r in range(0, rows + 2 * BORDER, BORDER):
                    total = None
                    for o in range(group):
                        who = posall[o]
                        row0, col0 = who[0:1, :width], who[1:2, :width]
                        inside = (cols >= col0) & (cols < col0 + n) & (line + r >= row0) & (line + r < row0 + n)
                        at_row = r % n
                        block = (rbuf[s, o, c, at_row:at_row + BORDER] if o
                                 else grad[at.block, s, c, at_row:at_row + BORDER])
                        term = jnp.where(inside, block.astype(F32), 0.0)
                        total = term if total is None else total + term
                    if away:
                        sbuf[s, c, r:r + BORDER, :] = total.astype(BF16)
                    else:
                        keep[s, c, r:r + BORDER, :] = total
            if away:
                ycopies[s] = remote(sbuf.at[s], ybuf.at[s], ysend.at[s], yrecv.at[s], at.partner)
                ycopies[s].start()
    first, last = at.tile == 0, at.tile == at.tiles - 1
    zcopies = {}
    for s in order:
        ycopies[s].wait_recv()
        for c in range(2):
            zout[s, 0, c] = (keep[s, c, :BORDER] + ybuf[s, c, :BORDER].astype(F32)).astype(BF16)
            zout[s, 1, c] = (keep[s, c, BORDER + rows:] + ybuf[s, c, BORDER + rows:].astype(F32)).astype(BF16)
        up = remote(zout.at[s, 0], zin.at[s, 0], zsend.at[s, 0], zrecv.at[s, 0], at.tile_peer(at.tiles - 1))
        down = remote(zout.at[s, 1], zin.at[s, 1], zsend.at[s, 1], zrecv.at[s, 1], at.tile_peer(1))
        zcopies[s] = (up, down)

        @pl.when(jnp.logical_not(first))
        def _():
            up.start()

        @pl.when(jnp.logical_not(last))
        def _():
            down.start()

        for c in range(2):
            for r in range(BORDER, BORDER + rows, BORDER):
                out[s, c, r - BORDER:r, :] = keep[s, c, r:r + BORDER] + ybuf[s, c, r:r + BORDER].astype(F32)
    for s in order:
        up, down = zcopies[s]

        @pl.when(jnp.logical_not(last))
        def _():
            up.wait_recv()
            for c in range(2):
                out[s, c, rows - BORDER:, :] += zin[s, 0, c].astype(F32)

        @pl.when(jnp.logical_not(first))
        def _():
            down.wait_recv()
            for c in range(2):
                out[s, c, :BORDER, :] += zin[s, 1, c].astype(F32)
            up.wait_send()

        @pl.when(jnp.logical_not(last))
        def _():
            down.wait_send()
    total = loss[...]
    for copy, o in zip(lcopies, range(1, at.tiles)):
        copy.wait_recv()
        total = total + lbuf[o]
    losses[...] = total
    for copy in list(xcopies.values()) + list(ycopies.values()) + lcopies:
        copy.wait_send()


def spread(grad, posall, loss, rows):
    group, slices, _, n, width = grad.shape
    tiles = lax.axis_size("tile")
    vmem = pl.BlockSpec(memory_space=pltpu.VMEM)
    dma = pltpu.SemaphoreType.DMA
    high = rows + 2 * BORDER
    return pl.pallas_call(
        functools.partial(spread_kernel, group),
        out_shape=(jax.ShapeDtypeStruct((slices, 2, rows, width), F32), jax.ShapeDtypeStruct((8, 128), F32)),
        in_specs=[vmem] * 3, out_specs=(vmem, vmem),
        scratch_shapes=[
            pltpu.VMEM((slices, group, 2, n, width), BF16), pltpu.VMEM((slices, 2, high, width), F32),
            pltpu.VMEM((slices, 2, high, width), BF16), pltpu.VMEM((slices, 2, high, width), BF16),
            pltpu.VMEM((slices, 2, 2, BORDER, width), BF16), pltpu.VMEM((slices, 2, 2, BORDER, width), BF16),
            pltpu.VMEM((tiles, 8, 128), F32),
            dma((tiles,)), dma((tiles,)), dma((slices, 2)), dma((slices, 2)), dma((slices,)), dma((slices,)),
            dma((slices, group)), dma((slices, group))],
        compiler_params=pltpu.CompilerParams(collective_id=1, has_side_effects=True, vmem_limit_bytes=24 << 20),
        name="spread",
    )(grad, posall, loss)


def extended(value, axis, dim, width):
    size, length = lax.axis_size(axis), value.shape[dim]
    up = [(i, i + 1) for i in range(size - 1)]
    down = [(j, i) for i, j in up]
    before = lax.ppermute(lax.slice_in_dim(value, length - width, length, axis=dim), axis, up)
    after = lax.ppermute(lax.slice_in_dim(value, 0, width, axis=dim), axis, down)
    return jnp.concatenate([before, value, after], axis=dim)


def fold_of(band, row0, col0, n, blocks):
    col, line = jnp.arange(n) < col0, (jnp.arange(n) < row0)[:, None]
    flat = jnp.where(col, band[..., n:], band[..., :n])
    over = jnp.pad(flat[..., n:, :], ((0, 0), (0, 0), (0, 2 * n - flat.shape[2]), (0, 0)))
    flat = jnp.where(line, over, flat[..., :n, :])
    return jnp.moveaxis(flat.reshape(flat.shape[:3] + (blocks, n // blocks)), 3, 0)


def unfold(grad, row0, col0, rows, cols):
    slices, n = grad.shape[1], grad.shape[3]
    flat = jnp.moveaxis(grad, 0, 3).reshape(slices, 2, n, n)
    r, c = jnp.arange(rows), jnp.arange(cols)
    inside = ((r >= row0) & (r < row0 + n))[:, None] & ((c >= col0) & (c < col0 + n))
    dense = jnp.concatenate([flat, flat[:, :, :rows - n]], axis=2)
    return jnp.where(inside, jnp.concatenate([dense, dense[..., :cols - n]], axis=3), 0)


def body(transmission, illumination, intensities, scan_positions, tile_owner):
    tile_index = lax.axis_index("tile")
    tile_rows, width = transmission.shape[2:]
    slots = tile_owner.shape[0]
    n = illumination.shape[-1]
    owned = tile_owner == tile_index
    chosen = jnp.sum(jnp.where(owned, jnp.arange(slots), 0)).astype(jnp.int32)
    usable = jnp.any(owned)
    place = jnp.sum(jnp.where(owned[:, None], scan_positions, 0), axis=0)
    pos = jnp.stack([place[0], place[1], usable.astype(jnp.int32), chosen])
    if width == 128 and lax.axis_size("probe") * width == 2 * n:
        postile = jnp.broadcast_to(jnp.pad(place, (0, 6))[:, None], (8, 128))
        fold, posall = collect(transmission, postile, n)
        grad, loss = compute(pos, fold, illumination, intensities)
        gradient, losses = spread(grad, posall, loss, tile_rows)
        return gradient, losses[:slots, 0]
    cols = lax.axis_size("probe") * width
    band = lax.all_gather(extended(transmission, "tile", 2, BORDER), "probe", axis=3, tiled=True)
    fold = fold_of(band, place[0], place[1], n, n // 128)
    grad, loss = compute(pos, fold, illumination, intensities)
    summed = unfold(grad, place[0], place[1], tile_rows + 2 * BORDER, cols)
    wide = lax.psum_scatter(summed, "probe", scatter_dimension=3, tiled=True).astype(F32)
    size = lax.axis_size("tile")
    up = [(i, i + 1) for i in range(size - 1)]
    down = [(j, i) for i, j in up]
    from_above = lax.ppermute(wide[:, :, :BORDER].astype(BF16), "tile", down).astype(F32)
    from_below = lax.ppermute(wide[:, :, tile_rows + BORDER:].astype(BF16), "tile", up).astype(F32)
    interior = wide[:, :, BORDER:BORDER + tile_rows]
    interior = interior.at[:, :, tile_rows - BORDER:].add(from_above)
    interior = interior.at[:, :, :BORDER].add(from_below)
    return interior, lax.psum(loss[:slots, 0], "tile")


def solution(mesh):
    in_specs = (P(None, None, "tile", "probe"), P(), P("probe", None, None), P("probe", None), P("probe"))
    out_specs = (P(None, None, "tile", "probe"), P("probe"))
    return jax.shard_map(body, mesh=mesh, in_specs=in_specs, out_specs=out_specs, check_vma=False)
```

```python
import functools
import math

import jax
import jax.numpy as jnp
import numpy as np
from jax import lax
from jax.experimental import pallas as pl
from jax.experimental.pallas import tpu as pltpu
from jax.sharding import PartitionSpec as P

BORDER = 128
FRESNEL = 0.25
F32 = jnp.float32
BF16 = jnp.bfloat16


def tables_of(n):
    k = np.arange(n)
    angle = -2.0 * np.pi * ((k[:, None] * k[None, :]) % n) / n
    wave = np.exp(1j * angle) / math.sqrt(n)
    freq = np.where(k < n // 2, k, k - n).astype(np.float64)
    h = np.exp(-1j * np.pi * FRESNEL * freq * freq / n)
    q = np.fft.ifft(h)
    prop = q[(k[:, None] - k[None, :]) % n]
    return [jnp.asarray(np.asarray(t, np.float32).astype(jnp.bfloat16))
            for t in (wave.real, wave.imag, prop.real, prop.imag)]


def compute_kernel(pos, fold, illum, meas, wr, wi, qr, qi, out, loss,
                   wide, x0, x1, obj, er, ei, ir, ii, msc, msem):
    n = illum.shape[-1]
    blocks, slices, width = fold.shape[0], fold.shape[1], fold.shape[-1]
    assert slices == 2
    step = n // 2
    row0, col0, usable, chosen = pos[0], pos[1], pos[2], pos[3]

    @pl.when(usable == 0)
    def _():
        loss[...] = jnp.zeros_like(loss)
        out[...] = jnp.zeros_like(out)

    def chunks(fn):
        def body(i, carry):
            fn(pl.multiple_of(i * step, step))
            return carry
        lax.fori_loop(0, n // step, body, 0)

    def transform(tr, ti, sign, emit):
        dot = functools.partial(jnp.dot, preferred_element_type=F32)

        def right(r):
            a, b = er[pl.ds(r, step), :], ei[pl.ds(r, step), :]
            rr, mm = dot(a, tr[...]), dot(b, ti[...])
            ir[pl.ds(r, step), :] = (rr - mm if sign > 0 else rr + mm).astype(BF16)
            rm, mr = dot(a, ti[...]), dot(b, tr[...])
            ii[pl.ds(r, step), :] = (mr + rm if sign > 0 else mr - rm).astype(BF16)

        chunks(right)

        def left(r):
            a, b = tr[pl.ds(r, step), :], ti[pl.ds(r, step), :]
            rr, mm = dot(a, ir[...]), dot(b, ii[...])
            rm, mr = dot(a, ii[...]), dot(b, ir[...])
            emit(r, rr - mm if sign > 0 else rr + mm, rm + mr if sign > 0 else rm - mr)

        chunks(left)

    @pl.when(usable != 0)
    def _():
        fetch = pltpu.make_async_copy(meas.at[chosen], msc, msem)
        fetch.start()
        wide[2 * n:, :] = jnp.zeros((8, n), F32)
        base = (n - row0) // 8 * 8
        turn = (72 - (n - row0 - base)) % 72
        for c in range(2):
            for r in range(0, n, 64):
                turned = pltpu.roll(illum[c, r:r + 64, :].astype(F32), col0 & (n - 1), 1)
                wide[r:r + 64, :] = turned
                wide[n + r:n + r + 64, :] = turned
            for r in range(0, n, 64):
                lines = wide[pl.ds(pl.multiple_of(base + r, 8), 72), :]
                x0[c, r:r + 64, :] = pltpu.roll(lines, turn, 0)[:64]

        for j in range(blocks):
            cols = slice(j * width, (j + 1) * width)
            for r in range(0, n, 128):
                rows = slice(r, r + 128)
                a, b = fold[j, 0, 0, rows].astype(F32), fold[j, 0, 1, rows].astype(F32)
                u, v = x0[0, rows, cols], x0[1, rows, cols]
                er[rows, cols] = (u * a - v * b).astype(BF16)
                ei[rows, cols] = (u * b + v * a).astype(BF16)
            obj[:, :, cols] = fold[j, 1]

        def emit_first(r, re, im):
            rows = pl.ds(r, step)
            x1[0, rows, :] = re
            x1[1, rows, :] = im
            a, b = obj[0, rows, :].astype(F32), obj[1, rows, :].astype(F32)
            er[rows, :] = (re * a - im * b).astype(BF16)
            ei[rows, :] = (re * b + im * a).astype(BF16)

        transform(qr, qi, 1, emit_first)
        fetch.wait()
        loss[...] = jnp.zeros_like(loss)

        def emit_far(r, re, im):
            rows = pl.ds(r, step)
            misfit = re * re + im * im - msc[rows, :]
            sq = jnp.sum((misfit * misfit).reshape(step // 8, 8, n), axis=0)
            loss[...] += functools.reduce(jnp.add, [sq[:, j:j + 128] for j in range(0, n, 128)])
            er[rows, :] = (misfit * re).astype(BF16)
            ei[rows, :] = (misfit * im).astype(BF16)

        transform(wr, wi, 1, emit_far)
        slot = lax.broadcasted_iota(jnp.int32, loss.shape, 0)
        loss[...] = jnp.where(slot == chosen, jnp.sum(loss[...]) / (n * n), 0.0)

        def place(s, r, parts):
            for c, g in enumerate(parts):
                for j in range(blocks):
                    out[j, s, c, pl.ds(r, step), :] = g[:, j * width:(j + 1) * width].astype(BF16)

        def emit_back(r, re, im):
            rows = pl.ds(r, step)
            u, v = x1[0, rows, :], x1[1, rows, :]
            place(1, r, (u * re + v * im, u * im - v * re))
            a, b = obj[0, rows, :].astype(F32), obj[1, rows, :].astype(F32)
            er[rows, :] = (a * re + b * im).astype(BF16)
            ei[rows, :] = (a * im - b * re).astype(BF16)

        transform(wr, wi, -1, emit_back)

        def emit_last(r, re, im):
            rows = pl.ds(r, step)
            u, v = x0[0, rows, :], x0[1, rows, :]
            place(0, r, (u * re + v * im, u * im - v * re))

        transform(qr, qi, -1, emit_last)


def compute(pos, fold, illumination, intensities):
    n = illumination.shape[-1]
    vmem = pl.BlockSpec(memory_space=pltpu.VMEM)
    return pl.pallas_call(
        compute_kernel,
        out_shape=(jax.ShapeDtypeStruct(fold.shape, BF16), jax.ShapeDtypeStruct((8, 128), F32)),
        in_specs=[pl.BlockSpec(memory_space=pltpu.SMEM), vmem, vmem,
                  pl.BlockSpec(memory_space=pl.ANY)] + [vmem] * 4,
        out_specs=(vmem, vmem),
        scratch_shapes=[
            pltpu.VMEM((2 * n + 8, n), F32), pltpu.VMEM((2, n, n), F32), pltpu.VMEM((2, n, n), F32),
            pltpu.VMEM((2, n, n), BF16)] + [pltpu.VMEM((n, n), BF16)] * 4 + [
            pltpu.VMEM((n, n), F32), pltpu.SemaphoreType.DMA],
        compiler_params=pltpu.CompilerParams(vmem_limit_bytes=40 << 20),
        name="probe_pass",
    )(pos, fold, illumination, intensities, *tables_of(n))


MESH = pl.DeviceIdType.MESH


class Places:
    def __init__(self, group):
        self.group, self.tiles = group, lax.axis_size("tile")
        self.me, self.tile = lax.axis_index("probe"), lax.axis_index("tile")
        self.half, self.block = self.me // group, lax.rem(self.me, group)
        self.partner = (lax.rem(self.me + group, 2 * group), self.tile)

    def peer(self, off):
        return (self.half * self.group + lax.rem(self.block + off, self.group), self.tile)

    def tile_peer(self, off):
        return (self.me, lax.rem(self.tile + off, self.tiles))

    def meet(self):
        barrier = pltpu.get_barrier_semaphore()
        others = ([self.partner] + [self.peer(o) for o in range(1, self.group)]
                  + [self.tile_peer(o) for o in range(1, self.tiles)])
        for other in others:
            pl.semaphore_signal(barrier, inc=1, device_id=other, device_id_type=MESH)
        pl.semaphore_wait(barrier, len(others))


def remote(src, dst, send, recv, device):
    return pltpu.make_async_remote_copy(src_ref=src, dst_ref=dst, send_sem=send, recv_sem=recv,
                                        device_id=device, device_id_type=MESH)


def fused_kernel(group, slots, tr, illum_hbm, meas_hbm, places, owners, wr_hbm, wi_hbm, qr_hbm, qi_hbm, out, losses,
                 ext, cbuf, fold, grad, rbuf, keep, sbuf, ybuf, zout, zin, pbuf, posall, loss, lbuf,
                 illum, meas, tables, x0, x1, er, ei, ir, ii,
                 local, psend, precv, zs, zr, msend, mrecv, ys, yr, xs, xr,
                 lsend, lrecv, zsend, zrecv, ysend, yrecv, xsend, xrecv):
    slices, _, rows, width = out.shape
    n = fold.shape[-2]
    extra = 2 * BORDER
    high = rows + extra
    step = n // 2
    dot = functools.partial(jnp.dot, preferred_element_type=F32)
    at = Places(group)
    first, last = at.tile == 0, at.tile == at.tiles - 1
    top, low, mid = slice(0, BORDER), slice(BORDER + rows, high), slice(BORDER, BORDER + rows)

    loads = [(tr.at[s], ext.at[s, 0, :, mid]) for s in range(slices)]
    loads += [(illum_hbm, illum), (qr_hbm, tables.at[0]), (qi_hbm, tables.at[1]), (wr_hbm, tables.at[2]),
              (wi_hbm, tables.at[3]), (meas_hbm, meas)]
    loads = [pltpu.make_async_copy(src, dst, local.at[i]) for i, (src, dst) in enumerate(loads)]
    for copy in loads:
        copy.start()
    owned = [owners[j] == at.tile for j in range(slots)]
    row0 = col0 = usable = chosen = jnp.int32(0)
    for j in range(slots):
        row0 = jnp.where(owned[j], places[j, 0], row0)
        col0 = jnp.where(owned[j], places[j, 1], col0)
        usable = jnp.where(owned[j], 1, usable)
        chosen = jnp.where(owned[j], j, chosen)
    sub = lax.broadcasted_iota(jnp.int32, (8, 128), 0)
    pbuf[...] = jnp.where(sub == 0, row0, col0)
    posall[0] = pbuf[...]
    at.meet()

    down = remote(tr.at[:, :, rows - BORDER:], ext.at[:, 0, :, top], zs.at[0], zr.at[0], at.tile_peer(1))
    up = remote(tr.at[:, :, :BORDER], ext.at[:, 0, :, low], zs.at[1], zr.at[1], at.tile_peer(at.tiles - 1))

    @pl.when(jnp.logical_not(last))
    def _():
        down.start()

    @pl.when(jnp.logical_not(first))
    def _():
        up.start()

    early = remote(tr.at[0, 0], ext.at[0, 1, 0, mid], msend, mrecv, at.partner)
    early.start()
    pcopies = [remote(pbuf, posall.at[o], psend.at[o], precv.at[o], at.peer(o)) for o in range(1, group)]
    for copy in pcopies:
        copy.start()

    @pl.when(first)
    def _():
        ext[:, 0, :, top, :] = jnp.zeros((slices, 2, BORDER, width), BF16)

    @pl.when(last)
    def _():
        ext[:, 0, :, low, :] = jnp.zeros((slices, 2, BORDER, width), BF16)

    for s in range(slices):
        loads[s].wait()

    @pl.when(jnp.logical_not(first))
    def _():
        down.wait_recv()

    @pl.when(jnp.logical_not(last))
    def _():
        up.wait_recv()

    yins = {}
    for s in range(slices):
        for c in range(2):
            parts = (top, low) if (s, c) == (0, 0) else (slice(0, high),)
            yins[s, c] = [remote(ext.at[s, 0, c, p], ext.at[s, 1, c, p], ys.at[s, c, i], yr.at[s, c, i], at.partner)
                          for i, p in enumerate(parts)]
            for copy in yins[s, c]:
                copy.start()
    yins[0, 0].append(early)

    loads[slices].wait()
    i = lax.broadcasted_iota(jnp.int32, (n, n), 0)
    j = lax.broadcasted_iota(jnp.int32, (n, n), 1)
    for target, line, lands, by in ((er, i, j, col0), (ei, j, i, row0)):
        moved = line + by
        target[...] = jnp.where(jnp.where(moved >= n, moved - n, moved) == lands, 1.0, 0.0).astype(BF16)
    for c in range(2):
        ir[...] = dot(illum[c], er[...]).astype(BF16)
        x0[c] = dot(ei[...], ir[...])

    for copy in pcopies:
        copy.wait_recv()
    lane = lax.broadcasted_iota(jnp.int32, (extra, width), 1) + at.block * width
    line = lax.broadcasted_iota(jnp.int32, (extra, width), 0)
    xins = {}
    for s in range(slices):
        for c in range(2):
            for copy in yins[s, c]:
                copy.wait_recv()
            for o in list(range(1, group)) + [0]:
                who = posall[(group - o) % group]
                prow, pcol = who[0:1, :width], who[1:2, :width]
                mine = jnp.where(lane < pcol, 1, 0) == at.half
                for r in range(0, n, extra):
                    v = jnp.where(mine, ext[s, 0, c, r:r + extra].astype(F32), ext[s, 1, c, r:r + extra].astype(F32))
                    if r + n < high:
                        w = jnp.where(mine, ext[s, 0, c, n + r:n + r + extra].astype(F32),
                                      ext[s, 1, c, n + r:n + r + extra].astype(F32))
                        v = jnp.where(line + r < prow, w, v)
                    if o:
                        cbuf[s, c, o, r:r + extra, :] = v.astype(BF16)
                    else:
                        fold[s, c, at.block, r:r + extra, :] = v.astype(BF16)
                if o:
                    xins[s, c, o] = remote(cbuf.at[s, c, o], fold.at[s, c, at.block], xs.at[s, c, o], xr.at[s, c, o],
                                           at.peer(o))
                    xins[s, c, o].start()

    def chunks(fn):
        def step_of(k, carry):
            fn(pl.multiple_of(k * step, step))
            return carry
        lax.fori_loop(0, n // step, step_of, 0)

    def transform(tr_at, ti_at, sign, emit):
        t_re, t_im = tables.at[tr_at], tables.at[ti_at]

        def right(r):
            a, b = er[pl.ds(r, step), :], ei[pl.ds(r, step), :]
            rr, mm = dot(a, t_re[...]), dot(b, t_im[...])
            ir[pl.ds(r, step), :] = (rr - mm if sign > 0 else rr + mm).astype(BF16)
            rm, mr = dot(a, t_im[...]), dot(b, t_re[...])
            ii[pl.ds(r, step), :] = (mr + rm if sign > 0 else mr - rm).astype(BF16)

        chunks(right)

        def left(r):
            a, b = t_re[pl.ds(r, step), :], t_im[pl.ds(r, step), :]
            rr, mm = dot(a, ir[...]), dot(b, ii[...])
            rm, mr = dot(a, ii[...]), dot(b, ir[...])
            emit(r, rr - mm if sign > 0 else rr + mm, rm + mr if sign > 0 else rm - mr)

        chunks(left)

    def exit_wave(s, wave):
        for c in range(2):
            for o in range(1, group):
                xins[s, c, o].wait_recv()
        for b in range(group):
            cols = slice(b * width, (b + 1) * width)
            for r in range(0, n, 128):
                part = slice(r, r + 128)
                p, q = fold[s, 0, b, part].astype(F32), fold[s, 1, b, part].astype(F32)
                u, v = wave[0, part, cols], wave[1, part, cols]
                er[part, cols] = (u * p - v * q).astype(BF16)
                ei[part, cols] = (u * q + v * p).astype(BF16)

    for copy in loads[slices + 1:slices + 3]:
        copy.wait()
    exit_wave(0, x0)

    def emit_first(r, re, im):
        x1[0, pl.ds(r, step), :] = re
        x1[1, pl.ds(r, step), :] = im

    transform(0, 1, 1, emit_first)
    for copy in loads[slices + 3:]:
        copy.wait()
    exit_wave(1, x1)
    loss[...] = jnp.zeros_like(loss)

    def emit_far(r, re, im):
        part = pl.ds(r, step)
        measured = meas[0, part, :]
        for k in range(1, slots):
            measured = jnp.where(chosen == k, meas[k, part, :], measured)
        misfit = jnp.where(usable == 1, re * re + im * im - measured, 0.0)
        sq = jnp.sum((misfit * misfit).reshape(step // 8, 8, n), axis=0)
        loss[...] += functools.reduce(jnp.add, [sq[:, k:k + 128] for k in range(0, n, 128)])
        er[part, :] = (misfit * re).astype(BF16)
        ei[part, :] = (misfit * im).astype(BF16)

    transform(2, 3, 1, emit_far)
    loss[...] = jnp.where(sub == chosen, jnp.sum(loss[...]) / (n * n), 0.0)

    def place(s, r, wave, re, im):
        u, v = wave[0, pl.ds(r, step), :], wave[1, pl.ds(r, step), :]
        for c, g in enumerate((u * re + v * im, u * im - v * re)):
            for b in range(group):
                grad[s, c, b, pl.ds(r, step), :] = g[:, b * width:(b + 1) * width].astype(BF16)

    def emit_back(r, re, im):
        part = pl.ds(r, step)
        place(1, r, x1, re, im)
        for b in range(group):
            cols = slice(b * width, (b + 1) * width)
            p, q = fold[1, 0, b, part, :].astype(F32), fold[1, 1, b, part, :].astype(F32)
            er[part, cols] = (p * re[:, cols] + q * im[:, cols]).astype(BF16)
            ei[part, cols] = (p * im[:, cols] - q * re[:, cols]).astype(BF16)

    xouts = {}

    def send(s):
        for c in range(2):
            for o in range(1, group):
                peer = lax.rem(at.block + o, group)
                xouts[s, c, o] = remote(grad.at[s, c, peer], rbuf.at[s, c, o], xsend.at[s, c, o], xrecv.at[s, c, o],
                                        at.peer(o))
                xouts[s, c, o].start()

    transform(2, 3, -1, emit_back)
    send(1)
    lcopies = [remote(loss, lbuf.at[o], lsend.at[o], lrecv.at[o], at.tile_peer(o)) for o in range(1, at.tiles)]
    for copy in lcopies:
        copy.start()
    transform(0, 1, -1, lambda r, re, im: place(0, r, x0, re, im))
    send(0)

    lane = lax.broadcasted_iota(jnp.int32, (BORDER, width), 1) + at.block * width
    line = lax.broadcasted_iota(jnp.int32, (BORDER, width), 0)
    order = [(s, c) for s in range(slices - 1, -1, -1) for c in range(2)]
    youts, zouts = {}, {}

    def add_up(s, c, away):
        cols = lane + (1 - at.half if away else at.half) * n
        for r in range(0, high, BORDER):
            total = None
            for o in range(group):
                who = posall[o]
                prow, pcol = who[0:1, :width], who[1:2, :width]
                inside = (cols >= pcol) & (cols < pcol + n) & (line + r >= prow) & (line + r < prow + n)
                k = r % n
                block = rbuf[s, c, o, k:k + BORDER] if o else grad[s, c, at.block, k:k + BORDER]
                term = jnp.where(inside, block.astype(F32), 0.0)
                total = term if total is None else total + term
            if away:
                sbuf[s, c, r:r + BORDER, :] = total.astype(BF16)
            else:
                keep[s, c, r:r + BORDER, :] = total

    def settle(s, c):
        youts[s, c].wait_recv()
        zout[s, c, 0] = (keep[s, c, top] + ybuf[s, c, top].astype(F32)).astype(BF16)
        zout[s, c, 1] = (keep[s, c, low] + ybuf[s, c, low].astype(F32)).astype(BF16)
        above = remote(zout.at[s, c, 0], zin.at[s, c, 0], zsend.at[s, c, 0], zrecv.at[s, c, 0],
                       at.tile_peer(at.tiles - 1))
        below = remote(zout.at[s, c, 1], zin.at[s, c, 1], zsend.at[s, c, 1], zrecv.at[s, c, 1], at.tile_peer(1))
        zouts[s, c] = (above, below)

        @pl.when(jnp.logical_not(first))
        def _():
            above.start()

        @pl.when(jnp.logical_not(last))
        def _():
            below.start()

        for r in range(BORDER, BORDER + rows, BORDER):
            out[s, c, r - BORDER:r, :] = keep[s, c, r:r + BORDER] + ybuf[s, c, r:r + BORDER].astype(F32)

    for k, (s, c) in enumerate(order):
        for o in range(1, group):
            xouts[s, c, o].wait_recv()
        add_up(s, c, True)
        youts[s, c] = remote(sbuf.at[s, c], ybuf.at[s, c], ysend.at[s, c], yrecv.at[s, c], at.partner)
        youts[s, c].start()
        add_up(s, c, False)
        if k:
            settle(*order[k - 1])
    settle(*order[-1])
    for s, c in order:
        above, below = zouts[s, c]

        @pl.when(jnp.logical_not(last))
        def _():
            above.wait_recv()
            out[s, c, rows - BORDER:, :] += zin[s, c, 0].astype(F32)

        @pl.when(jnp.logical_not(first))
        def _():
            below.wait_recv()
            out[s, c, :BORDER, :] += zin[s, c, 1].astype(F32)
            above.wait_send()

        @pl.when(jnp.logical_not(last))
        def _():
            below.wait_send()

    total = loss[...]
    for o, copy in zip(range(1, at.tiles), lcopies):
        copy.wait_recv()
        total = total + lbuf[o]
    losses[...] = total

    @pl.when(jnp.logical_not(last))
    def _():
        down.wait_send()

    @pl.when(jnp.logical_not(first))
    def _():
        up.wait_send()

    for copy in pcopies + lcopies + [c for pair in yins.values() for c in pair]:
        copy.wait_send()
    for group_of in (xins, xouts, youts):
        for copy in group_of.values():
            copy.wait_send()


def fused(transmission, illumination, intensities, scan_positions, tile_owner):
    slices, _, rows, width = transmission.shape
    n, slots = illumination.shape[-1], tile_owner.shape[0]
    group, tiles = n // width, lax.axis_size("tile")
    high = rows + 2 * BORDER
    vmem, smem, hbm = (pl.BlockSpec(memory_space=m) for m in (pltpu.VMEM, pltpu.SMEM, pl.ANY))
    dma = pltpu.SemaphoreType.DMA
    pair = (slices, 2)

    def buf(*shape, dtype=BF16):
        return pltpu.VMEM(shape, dtype)

    return pl.pallas_call(
        functools.partial(fused_kernel, group, slots),
        out_shape=(jax.ShapeDtypeStruct((slices, 2, rows, width), F32), jax.ShapeDtypeStruct((8, 128), F32)),
        in_specs=[hbm, hbm, hbm, smem, smem] + [hbm] * 4, out_specs=(vmem, vmem),
        scratch_shapes=[
            buf(slices, 2, 2, high, width), buf(*pair, group, n, width), buf(*pair, group, n, width),
            buf(*pair, group, n, width), buf(*pair, group, n, width), buf(*pair, high, width, dtype=F32),
            buf(*pair, high, width), buf(*pair, high, width), buf(*pair, 2, BORDER, width),
            buf(*pair, 2, BORDER, width), buf(8, 128, dtype=jnp.int32), buf(group, 8, 128, dtype=jnp.int32),
            buf(8, 128, dtype=F32), buf(tiles, 8, 128, dtype=F32),
            buf(2, n, n), buf(slots, n, n, dtype=F32), buf(4, n, n), buf(2, n, n, dtype=F32), buf(2, n, n, dtype=F32),
            buf(n, n), buf(n, n), buf(n, n), buf(n, n),
            dma((slices + 6,)), dma((group,)), dma((group,)), dma((2,)), dma((2,)), dma, dma,
            dma(pair + (2,)), dma(pair + (2,)), dma(pair + (group,)), dma(pair + (group,)),
            dma((tiles,)), dma((tiles,)), dma(pair + (2,)), dma(pair + (2,)), dma(pair), dma(pair),
            dma(pair + (group,)), dma(pair + (group,))],
        compiler_params=pltpu.CompilerParams(collective_id=0, has_side_effects=True, vmem_limit_bytes=60 << 20),
        name="fused_step",
    )(transmission, illumination, intensities, scan_positions, tile_owner, *tables_of(n))


def extended(value, axis, dim, width):
    size, length = lax.axis_size(axis), value.shape[dim]
    up = [(i, i + 1) for i in range(size - 1)]
    down = [(j, i) for i, j in up]
    before = lax.ppermute(lax.slice_in_dim(value, length - width, length, axis=dim), axis, up)
    after = lax.ppermute(lax.slice_in_dim(value, 0, width, axis=dim), axis, down)
    return jnp.concatenate([before, value, after], axis=dim)


def fold_of(band, row0, col0, n, blocks):
    col, line = jnp.arange(n) < col0, (jnp.arange(n) < row0)[:, None]
    flat = jnp.where(col, band[..., n:], band[..., :n])
    over = jnp.pad(flat[..., n:, :], ((0, 0), (0, 0), (0, 2 * n - flat.shape[2]), (0, 0)))
    flat = jnp.where(line, over, flat[..., :n, :])
    return jnp.moveaxis(flat.reshape(flat.shape[:3] + (blocks, n // blocks)), 3, 0)


def unfold(grad, row0, col0, rows, cols):
    slices, n = grad.shape[1], grad.shape[3]
    flat = jnp.moveaxis(grad, 0, 3).reshape(slices, 2, n, n)
    r, c = jnp.arange(rows), jnp.arange(cols)
    inside = ((r >= row0) & (r < row0 + n))[:, None] & ((c >= col0) & (c < col0 + n))
    dense = jnp.concatenate([flat, flat[:, :, :rows - n]], axis=2)
    return jnp.where(inside, jnp.concatenate([dense, dense[..., :cols - n]], axis=3), 0)


def body(transmission, illumination, intensities, scan_positions, tile_owner):
    tile_index = lax.axis_index("tile")
    tile_rows, width = transmission.shape[2:]
    slots = tile_owner.shape[0]
    n = illumination.shape[-1]
    owned = tile_owner == tile_index
    chosen = jnp.sum(jnp.where(owned, jnp.arange(slots), 0)).astype(jnp.int32)
    usable = jnp.any(owned)
    place = jnp.sum(jnp.where(owned[:, None], scan_positions, 0), axis=0)
    pos = jnp.stack([place[0], place[1], usable.astype(jnp.int32), chosen])
    if width == 128 and lax.axis_size("probe") * width == 2 * n:
        gradient, losses = fused(transmission, illumination, intensities, scan_positions, tile_owner)
        return gradient, losses[:slots, 0]
    cols = lax.axis_size("probe") * width
    band = lax.all_gather(extended(transmission, "tile", 2, BORDER), "probe", axis=3, tiled=True)
    fold = fold_of(band, place[0], place[1], n, n // 128)
    grad, loss = compute(pos, fold, illumination, intensities)
    summed = unfold(grad, place[0], place[1], tile_rows + 2 * BORDER, cols)
    wide = lax.psum_scatter(summed, "probe", scatter_dimension=3, tiled=True).astype(F32)
    size = lax.axis_size("tile")
    up = [(i, i + 1) for i in range(size - 1)]
    down = [(j, i) for i, j in up]
    from_above = lax.ppermute(wide[:, :, :BORDER].astype(BF16), "tile", down).astype(F32)
    from_below = lax.ppermute(wide[:, :, tile_rows + BORDER:].astype(BF16), "tile", up).astype(F32)
    interior = wide[:, :, BORDER:BORDER + tile_rows]
    interior = interior.at[:, :, tile_rows - BORDER:].add(from_above)
    interior = interior.at[:, :, :BORDER].add(from_below)
    return interior, lax.psum(loss[:slots, 0], "tile")


def solution(mesh):
    in_specs = (P(None, None, "tile", "probe"), P(), P("probe", None, None), P("probe", None), P("probe"))
    out_specs = (P(None, None, "tile", "probe"), P("probe"))
    return jax.shard_map(body, mesh=mesh, in_specs=in_specs, out_specs=out_specs, check_vma=False)
```

```python
import functools
import math

import jax
import jax.numpy as jnp
import numpy as np
from jax import lax
from jax.experimental import pallas as pl
from jax.experimental.pallas import tpu as pltpu
from jax.sharding import PartitionSpec as P

BORDER = 128
FRESNEL = 0.25
F32 = jnp.float32
BF16 = jnp.bfloat16


def tables_of(n):
    k = np.arange(n)
    angle = -2.0 * np.pi * ((k[:, None] * k[None, :]) % n) / n
    wave = np.exp(1j * angle) / math.sqrt(n)
    freq = np.where(k < n // 2, k, k - n).astype(np.float64)
    h = np.exp(-1j * np.pi * FRESNEL * freq * freq / n)
    q = np.fft.ifft(h)
    prop = q[(k[:, None] - k[None, :]) % n]
    return [jnp.asarray(np.asarray(t, np.float32).astype(jnp.bfloat16))
            for t in (wave.real, wave.imag, prop.real, prop.imag)]


def compute_kernel(pos, fold, illum, meas, wr, wi, qr, qi, out, loss,
                   wide, x0, x1, obj, er, ei, ir, ii, msc, msem):
    n = illum.shape[-1]
    blocks, slices, width = fold.shape[0], fold.shape[1], fold.shape[-1]
    assert slices == 2
    step = n // 2
    row0, col0, usable, chosen = pos[0], pos[1], pos[2], pos[3]

    @pl.when(usable == 0)
    def _():
        loss[...] = jnp.zeros_like(loss)
        out[...] = jnp.zeros_like(out)

    def chunks(fn):
        def body(i, carry):
            fn(pl.multiple_of(i * step, step))
            return carry
        lax.fori_loop(0, n // step, body, 0)

    def transform(tr, ti, sign, emit):
        dot = functools.partial(jnp.dot, preferred_element_type=F32)

        def right(r):
            a, b = er[pl.ds(r, step), :], ei[pl.ds(r, step), :]
            rr, mm = dot(a, tr[...]), dot(b, ti[...])
            ir[pl.ds(r, step), :] = (rr - mm if sign > 0 else rr + mm).astype(BF16)
            rm, mr = dot(a, ti[...]), dot(b, tr[...])
            ii[pl.ds(r, step), :] = (mr + rm if sign > 0 else mr - rm).astype(BF16)

        chunks(right)

        def left(r):
            a, b = tr[pl.ds(r, step), :], ti[pl.ds(r, step), :]
            rr, mm = dot(a, ir[...]), dot(b, ii[...])
            rm, mr = dot(a, ii[...]), dot(b, ir[...])
            emit(r, rr - mm if sign > 0 else rr + mm, rm + mr if sign > 0 else rm - mr)

        chunks(left)

    @pl.when(usable != 0)
    def _():
        fetch = pltpu.make_async_copy(meas.at[chosen], msc, msem)
        fetch.start()
        wide[2 * n:, :] = jnp.zeros((8, n), F32)
        base = (n - row0) // 8 * 8
        turn = (72 - (n - row0 - base)) % 72
        for c in range(2):
            for r in range(0, n, 64):
                turned = pltpu.roll(illum[c, r:r + 64, :].astype(F32), col0 & (n - 1), 1)
                wide[r:r + 64, :] = turned
                wide[n + r:n + r + 64, :] = turned
            for r in range(0, n, 64):
                lines = wide[pl.ds(pl.multiple_of(base + r, 8), 72), :]
                x0[c, r:r + 64, :] = pltpu.roll(lines, turn, 0)[:64]

        for j in range(blocks):
            cols = slice(j * width, (j + 1) * width)
            for r in range(0, n, 128):
                rows = slice(r, r + 128)
                a, b = fold[j, 0, 0, rows].astype(F32), fold[j, 0, 1, rows].astype(F32)
                u, v = x0[0, rows, cols], x0[1, rows, cols]
                er[rows, cols] = (u * a - v * b).astype(BF16)
                ei[rows, cols] = (u * b + v * a).astype(BF16)
            obj[:, :, cols] = fold[j, 1]

        def emit_first(r, re, im):
            rows = pl.ds(r, step)
            x1[0, rows, :] = re
            x1[1, rows, :] = im
            a, b = obj[0, rows, :].astype(F32), obj[1, rows, :].astype(F32)
            er[rows, :] = (re * a - im * b).astype(BF16)
            ei[rows, :] = (re * b + im * a).astype(BF16)

        transform(qr, qi, 1, emit_first)
        fetch.wait()
        loss[...] = jnp.zeros_like(loss)

        def emit_far(r, re, im):
            rows = pl.ds(r, step)
            misfit = re * re + im * im - msc[rows, :]
            sq = jnp.sum((misfit * misfit).reshape(step // 8, 8, n), axis=0)
            loss[...] += functools.reduce(jnp.add, [sq[:, j:j + 128] for j in range(0, n, 128)])
            er[rows, :] = (misfit * re).astype(BF16)
            ei[rows, :] = (misfit * im).astype(BF16)

        transform(wr, wi, 1, emit_far)
        slot = lax.broadcasted_iota(jnp.int32, loss.shape, 0)
        loss[...] = jnp.where(slot == chosen, jnp.sum(loss[...]) / (n * n), 0.0)

        def place(s, r, parts):
            for c, g in enumerate(parts):
                for j in range(blocks):
                    out[j, s, c, pl.ds(r, step), :] = g[:, j * width:(j + 1) * width].astype(BF16)

        def emit_back(r, re, im):
            rows = pl.ds(r, step)
            u, v = x1[0, rows, :], x1[1, rows, :]
            place(1, r, (u * re + v * im, u * im - v * re))
            a, b = obj[0, rows, :].astype(F32), obj[1, rows, :].astype(F32)
            er[rows, :] = (a * re + b * im).astype(BF16)
            ei[rows, :] = (a * im - b * re).astype(BF16)

        transform(wr, wi, -1, emit_back)

        def emit_last(r, re, im):
            rows = pl.ds(r, step)
            u, v = x0[0, rows, :], x0[1, rows, :]
            place(0, r, (u * re + v * im, u * im - v * re))

        transform(qr, qi, -1, emit_last)


def compute(pos, fold, illumination, intensities):
    n = illumination.shape[-1]
    vmem = pl.BlockSpec(memory_space=pltpu.VMEM)
    return pl.pallas_call(
        compute_kernel,
        out_shape=(jax.ShapeDtypeStruct(fold.shape, BF16), jax.ShapeDtypeStruct((8, 128), F32)),
        in_specs=[pl.BlockSpec(memory_space=pltpu.SMEM), vmem, vmem,
                  pl.BlockSpec(memory_space=pl.ANY)] + [vmem] * 4,
        out_specs=(vmem, vmem),
        scratch_shapes=[
            pltpu.VMEM((2 * n + 8, n), F32), pltpu.VMEM((2, n, n), F32), pltpu.VMEM((2, n, n), F32),
            pltpu.VMEM((2, n, n), BF16)] + [pltpu.VMEM((n, n), BF16)] * 4 + [
            pltpu.VMEM((n, n), F32), pltpu.SemaphoreType.DMA],
        compiler_params=pltpu.CompilerParams(vmem_limit_bytes=40 << 20),
        name="probe_pass",
    )(pos, fold, illumination, intensities, *tables_of(n))


MESH = pl.DeviceIdType.MESH


class Places:
    def __init__(self, group):
        self.group, self.tiles = group, lax.axis_size("tile")
        self.me, self.tile = lax.axis_index("probe"), lax.axis_index("tile")
        self.half, self.block = self.me // group, lax.rem(self.me, group)
        self.partner = (lax.rem(self.me + group, 2 * group), self.tile)

    def peer(self, off):
        return (self.half * self.group + lax.rem(self.block + off, self.group), self.tile)

    def tile_peer(self, off):
        return (self.me, lax.rem(self.tile + off, self.tiles))

    def meet(self):
        barrier = pltpu.get_barrier_semaphore()
        others = ([self.partner] + [self.peer(o) for o in range(1, self.group)]
                  + [self.tile_peer(o) for o in range(1, self.tiles)])
        for other in others:
            pl.semaphore_signal(barrier, inc=1, device_id=other, device_id_type=MESH)
        pl.semaphore_wait(barrier, len(others))


def remote(src, dst, send, recv, device):
    return pltpu.make_async_remote_copy(src_ref=src, dst_ref=dst, send_sem=send, recv_sem=recv,
                                        device_id=device, device_id_type=MESH)


def fused_kernel(group, slots, tr, illum_hbm, meas_hbm, places, owners, wr_hbm, wi_hbm, qr_hbm, qi_hbm, out, losses,
                 ext, cbuf, fold, grad, rbuf, keep, sbuf, ybuf, zout, zin, pbuf, posall, loss, lbuf,
                 illum, meas, tables, x0, x1, er, ei, ir, ii,
                 local, psend, precv, zs, zr, msend, mrecv, ys, yr, xs, xr,
                 lsend, lrecv, zsend, zrecv, ysend, yrecv, xsend, xrecv):
    slices, _, rows, width = out.shape
    n = fold.shape[-2]
    extra = 2 * BORDER
    high = rows + extra
    step = n // 2
    dot = functools.partial(jnp.dot, preferred_element_type=F32)
    at = Places(group)
    first, last = at.tile == 0, at.tile == at.tiles - 1
    top, low, mid = slice(0, BORDER), slice(BORDER + rows, high), slice(BORDER, BORDER + rows)

    loads = [(tr.at[s], ext.at[s, 0, :, mid]) for s in range(slices)]
    loads += [(illum_hbm, illum), (qr_hbm, tables.at[0]), (qi_hbm, tables.at[1]), (wr_hbm, tables.at[2]),
              (wi_hbm, tables.at[3]), (meas_hbm, meas)]
    loads = [pltpu.make_async_copy(src, dst, local.at[i]) for i, (src, dst) in enumerate(loads)]
    for copy in loads:
        copy.start()
    owned = [owners[j] == at.tile for j in range(slots)]
    row0 = col0 = usable = chosen = jnp.int32(0)
    for j in range(slots):
        row0 = jnp.where(owned[j], places[j, 0], row0)
        col0 = jnp.where(owned[j], places[j, 1], col0)
        usable = jnp.where(owned[j], 1, usable)
        chosen = jnp.where(owned[j], j, chosen)
    sub = lax.broadcasted_iota(jnp.int32, (8, 128), 0)
    pbuf[...] = jnp.where(sub == 0, row0, col0)
    posall[0] = pbuf[...]
    at.meet()

    down = remote(tr.at[:, :, rows - BORDER:], ext.at[:, 0, :, top], zs.at[0], zr.at[0], at.tile_peer(1))
    up = remote(tr.at[:, :, :BORDER], ext.at[:, 0, :, low], zs.at[1], zr.at[1], at.tile_peer(at.tiles - 1))

    @pl.when(jnp.logical_not(last))
    def _():
        down.start()

    @pl.when(jnp.logical_not(first))
    def _():
        up.start()

    early = remote(tr.at[0, 0], ext.at[0, 1, 0, mid], msend, mrecv, at.partner)
    early.start()
    pcopies = [remote(pbuf, posall.at[o], psend.at[o], precv.at[o], at.peer(o)) for o in range(1, group)]
    for copy in pcopies:
        copy.start()

    @pl.when(first)
    def _():
        ext[:, 0, :, top, :] = jnp.zeros((slices, 2, BORDER, width), BF16)

    @pl.when(last)
    def _():
        ext[:, 0, :, low, :] = jnp.zeros((slices, 2, BORDER, width), BF16)

    for s in range(slices):
        loads[s].wait()

    @pl.when(jnp.logical_not(first))
    def _():
        down.wait_recv()

    @pl.when(jnp.logical_not(last))
    def _():
        up.wait_recv()

    yins = {}
    for s in range(slices):
        for c in range(2):
            parts = (top, low) if (s, c) == (0, 0) else (slice(0, high),)
            yins[s, c] = [remote(ext.at[s, 0, c, p], ext.at[s, 1, c, p], ys.at[s, c, i], yr.at[s, c, i], at.partner)
                          for i, p in enumerate(parts)]
            for copy in yins[s, c]:
                copy.start()
    yins[0, 0].append(early)

    loads[slices].wait()
    i = lax.broadcasted_iota(jnp.int32, (n, n), 0)
    j = lax.broadcasted_iota(jnp.int32, (n, n), 1)
    for target, line, lands, by in ((er, i, j, col0), (ei, j, i, row0)):
        moved = line + by
        target[...] = jnp.where(jnp.where(moved >= n, moved - n, moved) == lands, 1.0, 0.0).astype(BF16)
    for c in range(2):
        ir[...] = dot(illum[c], er[...]).astype(BF16)
        x0[c] = dot(ei[...], ir[...])

    for copy in pcopies:
        copy.wait_recv()
    lane = lax.broadcasted_iota(jnp.int32, (extra, width), 1) + at.block * width
    line = lax.broadcasted_iota(jnp.int32, (extra, width), 0)
    xins = {}
    for s in range(slices):
        for c in range(2):
            for copy in yins[s, c]:
                copy.wait_recv()
            for o in list(range(1, group)) + [0]:
                who = posall[(group - o) % group]
                prow, pcol = who[0:1, :width], who[1:2, :width]
                mine = jnp.where(lane < pcol, 1, 0) == at.half
                for r in range(0, n, extra):
                    v = jnp.where(mine, ext[s, 0, c, r:r + extra].astype(F32), ext[s, 1, c, r:r + extra].astype(F32))
                    if r + n < high:
                        w = jnp.where(mine, ext[s, 0, c, n + r:n + r + extra].astype(F32),
                                      ext[s, 1, c, n + r:n + r + extra].astype(F32))
                        v = jnp.where(line + r < prow, w, v)
                    if o:
                        cbuf[s, c, o, r:r + extra, :] = v.astype(BF16)
                    else:
                        fold[s, c, at.block, r:r + extra, :] = v.astype(BF16)
                if o:
                    xins[s, c, o] = remote(cbuf.at[s, c, o], fold.at[s, c, at.block], xs.at[s, c, o], xr.at[s, c, o],
                                           at.peer(o))
                    xins[s, c, o].start()

    def chunks(fn):
        def step_of(k, carry):
            fn(pl.multiple_of(k * step, step))
            return carry
        lax.fori_loop(0, n // step, step_of, 0)

    def transform(tr_at, ti_at, sign, emit):
        t_re, t_im = tables.at[tr_at], tables.at[ti_at]

        def right(r):
            a, b = er[pl.ds(r, step), :], ei[pl.ds(r, step), :]
            rr, mm = dot(a, t_re[...]), dot(b, t_im[...])
            ir[pl.ds(r, step), :] = (rr - mm if sign > 0 else rr + mm).astype(BF16)
            rm, mr = dot(a, t_im[...]), dot(b, t_re[...])
            ii[pl.ds(r, step), :] = (mr + rm if sign > 0 else mr - rm).astype(BF16)

        chunks(right)

        def left(r):
            a, b = t_re[pl.ds(r, step), :], t_im[pl.ds(r, step), :]
            rr, mm = dot(a, ir[...]), dot(b, ii[...])
            rm, mr = dot(a, ii[...]), dot(b, ir[...])
            emit(r, rr - mm if sign > 0 else rr + mm, rm + mr if sign > 0 else rm - mr)

        chunks(left)

    def exit_wave(s, wave):
        for c in range(2):
            for o in range(1, group):
                xins[s, c, o].wait_recv()
        for b in range(group):
            cols = slice(b * width, (b + 1) * width)
            for r in range(0, n, 128):
                part = slice(r, r + 128)
                p, q = fold[s, 0, b, part].astype(F32), fold[s, 1, b, part].astype(F32)
                u, v = wave[0, part, cols], wave[1, part, cols]
                er[part, cols] = (u * p - v * q).astype(BF16)
                ei[part, cols] = (u * q + v * p).astype(BF16)

    for copy in loads[slices + 1:slices + 3]:
        copy.wait()
    exit_wave(0, x0)

    def emit_first(r, re, im):
        x1[0, pl.ds(r, step), :] = re
        x1[1, pl.ds(r, step), :] = im

    transform(0, 1, 1, emit_first)
    for copy in loads[slices + 3:]:
        copy.wait()
    exit_wave(1, x1)
    loss[...] = jnp.zeros_like(loss)

    def emit_far(r, re, im):
        part = pl.ds(r, step)
        measured = meas[0, part, :]
        for k in range(1, slots):
            measured = jnp.where(chosen == k, meas[k, part, :], measured)
        misfit = jnp.where(usable == 1, re * re + im * im - measured, 0.0)
        sq = jnp.sum((misfit * misfit).reshape(step // 8, 8, n), axis=0)
        loss[...] += functools.reduce(jnp.add, [sq[:, k:k + 128] for k in range(0, n, 128)])
        er[part, :] = (misfit * re).astype(BF16)
        ei[part, :] = (misfit * im).astype(BF16)

    transform(2, 3, 1, emit_far)
    loss[...] = jnp.where(sub == chosen, jnp.sum(loss[...]) / (n * n), 0.0)

    def place(s, r, wave, re, im):
        u, v = wave[0, pl.ds(r, step), :], wave[1, pl.ds(r, step), :]
        for c, g in enumerate((u * re + v * im, u * im - v * re)):
            for b in range(group):
                grad[s, c, b, pl.ds(r, step), :] = g[:, b * width:(b + 1) * width].astype(BF16)

    def emit_back(r, re, im):
        part = pl.ds(r, step)
        place(1, r, x1, re, im)
        for b in range(group):
            cols = slice(b * width, (b + 1) * width)
            p, q = fold[1, 0, b, part, :].astype(F32), fold[1, 1, b, part, :].astype(F32)
            er[part, cols] = (p * re[:, cols] + q * im[:, cols]).astype(BF16)
            ei[part, cols] = (p * im[:, cols] - q * re[:, cols]).astype(BF16)

    xouts = {}

    def send(s):
        for c, h in ((0, 0), (0, 1), (1, 0), (1, 1)):
            lines = slice(h * step, (h + 1) * step)
            for o in range(1, group):
                peer = lax.rem(at.block + o, group)
                xouts[s, c, h, o] = remote(grad.at[s, c, peer, lines], rbuf.at[s, c, o, lines], xsend.at[s, c, h, o],
                                           xrecv.at[s, c, h, o], at.peer(o))
                xouts[s, c, h, o].start()

    transform(2, 3, -1, emit_back)
    send(1)
    lcopies = [remote(loss, lbuf.at[o], lsend.at[o], lrecv.at[o], at.tile_peer(o)) for o in range(1, at.tiles)]
    for copy in lcopies:
        copy.start()
    transform(0, 1, -1, lambda r, re, im: place(0, r, x0, re, im))
    send(0)

    lane = lax.broadcasted_iota(jnp.int32, (BORDER, width), 1) + at.block * width
    line = lax.broadcasted_iota(jnp.int32, (BORDER, width), 0)
    order = [(s, c, h) for s in range(slices - 1, -1, -1) for c in range(2) for h in range(2)]
    spans = ((slice(0, step), slice(n, high)), (slice(step, n),))
    youts, zouts = {}, {}

    def add_up(s, c, h, away):
        cols = lane + (1 - at.half if away else at.half) * n
        for r in [r for p in spans[h] for r in range(p.start, p.stop, BORDER)]:
            total = None
            for o in range(group):
                who = posall[o]
                prow, pcol = who[0:1, :width], who[1:2, :width]
                inside = (cols >= pcol) & (cols < pcol + n) & (line + r >= prow) & (line + r < prow + n)
                k = r % n
                block = rbuf[s, c, o, k:k + BORDER] if o else grad[s, c, at.block, k:k + BORDER]
                term = jnp.where(inside, block.astype(F32), 0.0)
                total = term if total is None else total + term
            if away:
                sbuf[s, c, r:r + BORDER, :] = total.astype(BF16)
            else:
                keep[s, c, r:r + BORDER, :] = total

    def settle(s, c, h):
        for copy in youts[s, c, h]:
            copy.wait_recv()
        if h == 0:
            zout[s, c, 0] = (keep[s, c, top] + ybuf[s, c, top].astype(F32)).astype(BF16)
            zout[s, c, 1] = (keep[s, c, low] + ybuf[s, c, low].astype(F32)).astype(BF16)
            above = remote(zout.at[s, c, 0], zin.at[s, c, 0], zsend.at[s, c, 0], zrecv.at[s, c, 0],
                           at.tile_peer(at.tiles - 1))
            below = remote(zout.at[s, c, 1], zin.at[s, c, 1], zsend.at[s, c, 1], zrecv.at[s, c, 1], at.tile_peer(1))
            zouts[s, c] = (above, below)

            @pl.when(jnp.logical_not(first))
            def _():
                above.start()

            @pl.when(jnp.logical_not(last))
            def _():
                below.start()

        for r in [r for p in spans[h] for r in range(p.start, p.stop, BORDER) if BORDER <= r < BORDER + rows]:
            out[s, c, r - BORDER:r, :] = keep[s, c, r:r + BORDER] + ybuf[s, c, r:r + BORDER].astype(F32)

    for k, (s, c, h) in enumerate(order):
        for o in range(1, group):
            xouts[s, c, h, o].wait_recv()
        add_up(s, c, h, True)
        youts[s, c, h] = [remote(sbuf.at[s, c, p], ybuf.at[s, c, p], ysend.at[s, c, h + i * 2], yrecv.at[s, c, h + i * 2],
                                 at.partner) for i, p in enumerate(spans[h])]
        for copy in youts[s, c, h]:
            copy.start()
        add_up(s, c, h, False)
        if k:
            settle(*order[k - 1])
    settle(*order[-1])
    for s, c in zouts:
        above, below = zouts[s, c]

        @pl.when(jnp.logical_not(last))
        def _():
            above.wait_recv()
            out[s, c, rows - BORDER:, :] += zin[s, c, 0].astype(F32)

        @pl.when(jnp.logical_not(first))
        def _():
            below.wait_recv()
            out[s, c, :BORDER, :] += zin[s, c, 1].astype(F32)
            above.wait_send()

        @pl.when(jnp.logical_not(last))
        def _():
            below.wait_send()

    total = loss[...]
    for o, copy in zip(range(1, at.tiles), lcopies):
        copy.wait_recv()
        total = total + lbuf[o]
    losses[...] = total

    @pl.when(jnp.logical_not(last))
    def _():
        down.wait_send()

    @pl.when(jnp.logical_not(first))
    def _():
        up.wait_send()

    for copy in pcopies + lcopies + [c for pair in yins.values() for c in pair]:
        copy.wait_send()
    for copy in [c for pair in youts.values() for c in pair]:
        copy.wait_send()
    for group_of in (xins, xouts):
        for copy in group_of.values():
            copy.wait_send()


def fused(transmission, illumination, intensities, scan_positions, tile_owner):
    slices, _, rows, width = transmission.shape
    n, slots = illumination.shape[-1], tile_owner.shape[0]
    group, tiles = n // width, lax.axis_size("tile")
    high = rows + 2 * BORDER
    vmem, smem, hbm = (pl.BlockSpec(memory_space=m) for m in (pltpu.VMEM, pltpu.SMEM, pl.ANY))
    dma = pltpu.SemaphoreType.DMA
    pair = (slices, 2)

    def buf(*shape, dtype=BF16):
        return pltpu.VMEM(shape, dtype)

    return pl.pallas_call(
        functools.partial(fused_kernel, group, slots),
        out_shape=(jax.ShapeDtypeStruct((slices, 2, rows, width), F32), jax.ShapeDtypeStruct((8, 128), F32)),
        in_specs=[hbm, hbm, hbm, smem, smem] + [hbm] * 4, out_specs=(vmem, vmem),
        scratch_shapes=[
            buf(slices, 2, 2, high, width), buf(*pair, group, n, width), buf(*pair, group, n, width),
            buf(*pair, group, n, width), buf(*pair, group, n, width), buf(*pair, high, width, dtype=F32),
            buf(*pair, high, width), buf(*pair, high, width), buf(*pair, 2, BORDER, width),
            buf(*pair, 2, BORDER, width), buf(8, 128, dtype=jnp.int32), buf(group, 8, 128, dtype=jnp.int32),
            buf(8, 128, dtype=F32), buf(tiles, 8, 128, dtype=F32),
            buf(2, n, n), buf(slots, n, n, dtype=F32), buf(4, n, n), buf(2, n, n, dtype=F32), buf(2, n, n, dtype=F32),
            buf(n, n), buf(n, n), buf(n, n), buf(n, n),
            dma((slices + 6,)), dma((group,)), dma((group,)), dma((2,)), dma((2,)), dma, dma,
            dma(pair + (2,)), dma(pair + (2,)), dma(pair + (group,)), dma(pair + (group,)),
            dma((tiles,)), dma((tiles,)), dma(pair + (2,)), dma(pair + (2,)), dma(pair + (3,)), dma(pair + (3,)),
            dma(pair + (2, group)), dma(pair + (2, group))],
        compiler_params=pltpu.CompilerParams(collective_id=0, has_side_effects=True, vmem_limit_bytes=60 << 20),
        name="fused_step",
    )(transmission, illumination, intensities, scan_positions, tile_owner, *tables_of(n))


def extended(value, axis, dim, width):
    size, length = lax.axis_size(axis), value.shape[dim]
    up = [(i, i + 1) for i in range(size - 1)]
    down = [(j, i) for i, j in up]
    before = lax.ppermute(lax.slice_in_dim(value, length - width, length, axis=dim), axis, up)
    after = lax.ppermute(lax.slice_in_dim(value, 0, width, axis=dim), axis, down)
    return jnp.concatenate([before, value, after], axis=dim)


def fold_of(band, row0, col0, n, blocks):
    col, line = jnp.arange(n) < col0, (jnp.arange(n) < row0)[:, None]
    flat = jnp.where(col, band[..., n:], band[..., :n])
    over = jnp.pad(flat[..., n:, :], ((0, 0), (0, 0), (0, 2 * n - flat.shape[2]), (0, 0)))
    flat = jnp.where(line, over, flat[..., :n, :])
    return jnp.moveaxis(flat.reshape(flat.shape[:3] + (blocks, n // blocks)), 3, 0)


def unfold(grad, row0, col0, rows, cols):
    slices, n = grad.shape[1], grad.shape[3]
    flat = jnp.moveaxis(grad, 0, 3).reshape(slices, 2, n, n)
    r, c = jnp.arange(rows), jnp.arange(cols)
    inside = ((r >= row0) & (r < row0 + n))[:, None] & ((c >= col0) & (c < col0 + n))
    dense = jnp.concatenate([flat, flat[:, :, :rows - n]], axis=2)
    return jnp.where(inside, jnp.concatenate([dense, dense[..., :cols - n]], axis=3), 0)


def body(transmission, illumination, intensities, scan_positions, tile_owner):
    tile_index = lax.axis_index("tile")
    tile_rows, width = transmission.shape[2:]
    slots = tile_owner.shape[0]
    n = illumination.shape[-1]
    owned = tile_owner == tile_index
    chosen = jnp.sum(jnp.where(owned, jnp.arange(slots), 0)).astype(jnp.int32)
    usable = jnp.any(owned)
    place = jnp.sum(jnp.where(owned[:, None], scan_positions, 0), axis=0)
    pos = jnp.stack([place[0], place[1], usable.astype(jnp.int32), chosen])
    if width == 128 and lax.axis_size("probe") * width == 2 * n:
        gradient, losses = fused(transmission, illumination, intensities, scan_positions, tile_owner)
        return gradient, losses[:slots, 0]
    cols = lax.axis_size("probe") * width
    band = lax.all_gather(extended(transmission, "tile", 2, BORDER), "probe", axis=3, tiled=True)
    fold = fold_of(band, place[0], place[1], n, n // 128)
    grad, loss = compute(pos, fold, illumination, intensities)
    summed = unfold(grad, place[0], place[1], tile_rows + 2 * BORDER, cols)
    wide = lax.psum_scatter(summed, "probe", scatter_dimension=3, tiled=True).astype(F32)
    size = lax.axis_size("tile")
    up = [(i, i + 1) for i in range(size - 1)]
    down = [(j, i) for i, j in up]
    from_above = lax.ppermute(wide[:, :, :BORDER].astype(BF16), "tile", down).astype(F32)
    from_below = lax.ppermute(wide[:, :, tile_rows + BORDER:].astype(BF16), "tile", up).astype(F32)
    interior = wide[:, :, BORDER:BORDER + tile_rows]
    interior = interior.at[:, :, tile_rows - BORDER:].add(from_above)
    interior = interior.at[:, :, :BORDER].add(from_below)
    return interior, lax.psum(loss[:slots, 0], "tile")


def solution(mesh):
    in_specs = (P(None, None, "tile", "probe"), P(), P("probe", None, None), P("probe", None), P("probe"))
    out_specs = (P(None, None, "tile", "probe"), P("probe"))
    return jax.shard_map(body, mesh=mesh, in_specs=in_specs, out_specs=out_specs, check_vma=False)
```
